256 devices in a mesh: ta: 4 (over x_lo, core), ha: 4 (over y), wa: 16 (over x_hi, z).
Axes of the slice: x: 4 (x_hi: 2, x_lo: 2; x = x_hi * 2 + x_lo), y: 4, z: 8, core: 2. Of those that a mesh axis runs over, the one named last changes fastest.
Arguments:
- queries: bfloat16 [8, 64, 128, 2048], P('ta', 'ha', 'wa'), may hold values from -16 to 16
- keyvals: bfloat16 [2, 8, 64, 128, 2048], P(None, 'ta', 'ha', 'wa'), may hold values from -6 to 6
- far_frames: int32 [8, 8, 16, 2], P('ta', 'ha', 'wa'), may hold values from 0 to 7, as said below
Outputs:
- attended: bfloat16 [8, 64, 128, 2048], P('ta', 'ha', 'wa')
The draws below stay inside these ranges and needn't reach their ends.
Inputs may be any that keep to these rules, and one draw needn't show every extreme that they name: far_frames[t, a, b, :] are 2 different frames, each at a distance of 2 or more from t modulo 8.
All inputs are finite; a program needn't handle non-finite values.
Results may differ from the reference program's by a relative error of at most 0.0049.
Values may be sent and summed in bfloat16 or wider, within the bound.
A program may use at most 192 MiB of HBM per device.

```python
import jax
import jax.numpy as jnp
from jax import lax

TILE = 8
HEADS = 16
HD = 128
NFAR = 2
NF = 8
NH = 64
NW = 128


def base_keys(key):
    sample_key = jax.random.fold_in(key, 7)
    sampled = jnp.clip(jax.random.normal(sample_key, (NF, NH, NW, HEADS * HD), jnp.float32), -6.0, 6.0)
    return sampled


def draw_keyvals(key, part):
    sampled = base_keys(key)
    value_key = jax.random.fold_in(key, 8)
    key_part = sampled
    value_part = jnp.clip(jax.random.normal(value_key, (NF, NH, NW, HEADS * HD), jnp.float32), -6.0, 6.0)
    return jnp.stack([key_part, value_part]).astype(jnp.bfloat16)


def draw_queries(key, part):
    query_key = jax.random.fold_in(key, 9)
    result = 2.5 * jnp.clip(jax.random.normal(query_key, (NF, NH, NW, HEADS * HD), jnp.float32), -6.0, 6.0)
    return result.astype(jnp.bfloat16)


def draw_far_frames(key, part):
    shape_tiles = (NF, NH // TILE, NW // TILE)
    first_step = 2 + jax.random.randint(jax.random.fold_in(key, 21), shape_tiles, 0, NF - 3)
    extra_step = jax.random.randint(jax.random.fold_in(key, 22), shape_tiles, 1, NF - 3)
    second_step = 2 + (first_step - 2 + extra_step) % (NF - 3)
    frame_ids = jnp.arange(NF, dtype=jnp.int32)[:, None, None]
    return jnp.stack([(frame_ids + first_step) % NF, (frame_ids + second_step) % NF], axis=-1).astype(jnp.int32)


def setup_inputs(seed: int = 0) -> dict:
    splits = jax.random.split(jax.random.key(seed), 4)
    return {
        "queries": draw_queries(jax.random.fold_in(splits[3], 71), 0),
        "keyvals": draw_keyvals(jax.random.fold_in(splits[3], 71), 0),
        "far_frames": draw_far_frames(jax.random.fold_in(splits[3], 71), 0),
    }


def start_at(*values):
    return tuple(jnp.asarray(value).astype(jnp.int32) for value in values)


def reference(queries, keyvals, far_frames):
    tile_rows = NH // TILE
    tile_cols = NW // TILE
    features = HEADS * HD
    scaling = HD ** -0.5
    padded = jnp.pad(keyvals, ((0, 0), (0, 0), (TILE, TILE), (TILE, TILE), (0, 0)))
    offsets = jnp.arange(3 * TILE, dtype=jnp.int32) // TILE - 1

    def attend(tile_index):
        frame_at = tile_index // (tile_rows * tile_cols)
        row_at = (tile_index // tile_cols) % tile_rows
        column = tile_index % tile_cols
        query_rows = lax.dynamic_slice(queries, start_at(frame_at, row_at * TILE, column * TILE, 0), (1, TILE, TILE, features)).reshape(TILE * TILE, HEADS, HD)
        window = jnp.concatenate([lax.dynamic_slice(padded, start_at(0, (frame_at + time_step) % NF, row_at * TILE, column * TILE, 0), (2, 1, 3 * TILE, 3 * TILE, features)) for time_step in (-1, 0, 1)], axis=1)
        distant = jnp.concatenate([lax.dynamic_slice(keyvals, start_at(0, far_frames[frame_at, row_at, column, far_slot], row_at * TILE, column * TILE, 0), (2, 1, TILE, TILE, features)) for far_slot in range(NFAR)], axis=1)
        key_rows = jnp.concatenate([window[0].reshape(-1, HEADS, HD), distant[0].reshape(-1, HEADS, HD)], axis=0)
        values = jnp.concatenate([window[1].reshape(-1, HEADS, HD), distant[1].reshape(-1, HEADS, HD)], axis=0)
        row_valid = (row_at + offsets >= 0) & (row_at + offsets < tile_rows)
        column_valid = (column + offsets >= 0) & (column + offsets < tile_cols)
        inside = jnp.broadcast_to(row_valid[None, :, None] & column_valid[None, None, :], (3, 3 * TILE, 3 * TILE)).reshape(-1)
        inside = jnp.concatenate([inside, jnp.ones((NFAR * TILE * TILE,), dtype=bool)])
        scores = jnp.einsum("qhd,khd->hqk", query_rows.astype(jnp.float32), key_rows.astype(jnp.float32)) * scaling
        scores = jnp.where(inside[None, None, :], scores, jnp.float32(-1e30))
        peak_score = jnp.max(scores, axis=-1, keepdims=True)
        exponent = jnp.exp(scores - peak_score)
        denominator = jnp.sum(exponent, axis=-1, keepdims=True)
        normed = (exponent / denominator).astype(jnp.bfloat16)
        blended = jnp.einsum("hqk,khd->qhd", normed.astype(jnp.float32), values.astype(jnp.float32))
        return blended.reshape(TILE, TILE, features).astype(jnp.bfloat16)

    tile_outputs = lax.map(attend, jnp.arange(NF * tile_rows * tile_cols, dtype=jnp.int32))
    tile_outputs = tile_outputs.reshape(NF, tile_rows, tile_cols, TILE, TILE, features)
    return tile_outputs.transpose(0, 1, 3, 2, 4, 5).reshape(NF, NH, NW, features)
```

```python
import functools

import jax
import jax.numpy as jnp
from jax import lax
from jax.experimental import pallas as pl
from jax.experimental.pallas import tpu as pltpu
from jax.sharding import PartitionSpec as P

MESH = pl.DeviceIdType.MESH
HD = 128
NF = 8
ROWS = 128
EXP2_SCALE = HD**-0.5 * 1.4426950408889634
NEG = -1e30
NT = (((1,), (1,)), ((), ()))


def kernel(q, kv, far, out, *scratch):
    qs, own, left, right = (scratch[4 * i : 4 * i + 4] for i in range(4))
    (fars, bias, scores, probs, result, kv_send, kv_recv, q_send, q_recv, f_send, f_recv, z_send, z_recv, o_send, o_recv) = scratch[16:]
    ta, y, wa = lax.axis_index("ta"), lax.axis_index("ha"), lax.axis_index("wa")
    x_lo, core, x_hi, z = ta // 2, ta % 2, wa // 8, wa % 8
    x = x_hi * 2 + x_lo
    column = core * 8 + z
    has_left, has_right = column > 0, column < 15

    def place(px, pcore, py):
        return {"ta": (px % 2) * 2 + pcore, "ha": py, "wa": (px // 2) * 8 + z}

    def source(pta, py):
        return {"ta": pta, "ha": py, "wa": core * 8 + z}

    def beside(side):
        c = column + side
        return {"ta": x_lo * 2 + c // 8, "ha": y, "wa": x_hi * 8 + c % 8}

    def lanes(head):
        return pl.ds(pl.multiple_of(head * HD, HD), HD)

    barrier = pltpu.get_barrier_semaphore()

    @pl.loop(0, 16)
    def _(i):
        for device in (place(i // 4, x_hi, i % 4), source(i // 4, i % 4)):
            pl.semaphore_signal(barrier, inc=1, device_id=device, device_id_type=MESH)

    for side, there in ((-1, has_left), (1, has_right)):

        @pl.when(there)
        def _(side=side):
            pl.semaphore_signal(barrier, inc=1, device_id=beside(side), device_id_type=MESH)

    pl.semaphore_wait(barrier, 32 + has_left.astype(jnp.int32) + has_right.astype(jnp.int32))

    def kv_copy(k, dx):
        px, py = (x + dx) % 4, (y + k) % 4
        return (kv.at[:, :, :, lanes(px * 4 + py)], own[k].at[:, pl.ds(2 * ta, 2)], kv_send.at[4 * k + dx], kv_recv.at[4 * k + ta], px, py)

    def q_copy(k, dx):
        px, py = (x + dx) % 4, (y + k) % 4
        return (q.at[:, :, lanes(px * 4 + py)], qs[k].at[pl.ds(2 * ta, 2)], q_send.at[4 * k + dx], q_recv.at[4 * k + ta], px, py)

    def far_copy(k, dx):
        px, py = (x + dx) % 4, (y + k) % 4
        return (far, fars.at[4 * k + ta], f_send.at[4 * k + dx], f_recv.at[4 * k + ta], px, py)

    def remote(copy):
        src, dst, ss, rs, px, py = copy
        return pltpu.make_async_remote_copy(src, dst, ss, rs, device_id=place(px, x_hi, py), device_id_type=MESH)

    def exchange(make, k):
        src, dst, _, rs, _, _ = make(k, 0)
        if k == 0:

            @pl.when(core == x_hi)
            def _():
                pltpu.make_async_copy(src, dst, rs).start()

            @pl.when(core != x_hi)
            def _():
                remote(make(k, 0)).start()
        else:
            remote(make(k, 0)).start()

        @pl.loop(1, 4)
        def _(dx):
            remote(make(k, dx)).start()

    def exchanged(make, k):
        if k == 0:

            @pl.when(core != x_hi)
            def _():
                remote(make(k, 0)).wait_send()
        else:
            remote(make(k, 0)).wait_send()

        @pl.loop(1, 4)
        def _(dx):
            remote(make(k, dx)).wait_send()

    for k in range(4):
        exchange(far_copy, k)
    exchange(kv_copy, 0)
    exchange(kv_copy, 1)
    exchange(q_copy, 0)
    exchange(q_copy, 1)
    for k in (2, 3):
        exchange(kv_copy, k)
        exchange(q_copy, k)

    @pl.when(column == 0)
    def _():
        for ref in left:
            ref[...] = jnp.zeros_like(ref)

    @pl.when(column == 15)
    def _():
        for ref in right:
            ref[...] = jnp.zeros_like(ref)

    nearer = (((x - 2 * core + 3) % 4) < ((x - 2 * core + 4) % 4)).astype(jnp.int32)

    def piece(j):
        return ((nearer + j // 2) % 2) * 2 + j % 2

    def halo_copy(k, t, side):
        part = (slice(None), pl.ds(2 * t, 2))
        s = 0 if side < 0 else 1
        return pltpu.make_async_remote_copy(
            own[k].at[part],
            (right if side < 0 else left)[k].at[part],
            z_send.at[s, 4 * k + t],
            z_recv.at[s, 4 * k + t],
            device_id=beside(side),
            device_id_type=MESH,
        )

    def forward(k):
        @pl.loop(0, 4)
        def _(j):
            t = piece(j)
            pltpu.make_async_copy(own[k].at[:, pl.ds(2 * t, 2)], own[k].at[:, pl.ds(2 * t, 2)], kv_recv.at[4 * k + t]).wait()
            for side, there in ((1, has_right), (-1, has_left)):

                @pl.when(there)
                def _(side=side):
                    halo_copy(k, t, side).start()

    def arrived(k):
        @pl.loop(0, 4)
        def _(t):
            @pl.when(has_left)
            def _():
                halo_copy(k, t, 1).wait_recv()

            @pl.when(has_right)
            def _():
                halo_copy(k, t, -1).wait_recv()

            pltpu.make_async_copy(qs[k].at[pl.ds(2 * t, 2)], qs[k].at[pl.ds(2 * t, 2)], q_recv.at[4 * k + t]).wait()
            pltpu.make_async_copy(far, fars.at[4 * k + t], f_recv.at[4 * k + t]).wait()

    def set_bias(k):
        wraps = (y == k).astype(jnp.int32)
        row = lax.broadcasted_iota(jnp.int32, (ROWS, 2 * ROWS), 0)
        key = lax.broadcasted_iota(jnp.int32, (ROWS, 2 * ROWS), 1)
        half = row // 64
        base = jnp.where((key >= half * (64 + 64 * wraps)) & (key < 192 - 64 * wraps + half * 256), 0.0, NEG).astype(jnp.float32)
        bias[1] = base
        bias[0] = jnp.where(has_left, base, NEG)
        bias[2] = jnp.where(has_right, base, NEG)
        bias[3] = jnp.where(half == key // 128, 0.0, NEG).astype(jnp.float32)

    def unit(k, t):
        low = (k + 1) % 4
        query = jnp.concatenate([qs[low][t, 64:, :], qs[k][t, :64, :]], axis=0)
        around = [(t + 7) % NF, t, (t + 1) % NF]
        f_low, f_here = 4 * low + t // 2, 4 * k + t // 2
        f_at = (t % 2) * 4
        distant = [fars[f_low, f_at + 2], fars[f_low, f_at + 3], fars[f_here, f_at], fars[f_here, f_at + 1]]

        def rows(kind):
            chunks = []
            for side, cells in enumerate((left, own, right)):
                for f in around:
                    chunks.append((side, lambda cells=cells, f=f: jnp.concatenate([cells[low][kind, f], cells[k][kind, f]], axis=0)))
            chunks.append(
                (
                    3,
                    lambda: jnp.concatenate(
                        [
                            own[low][kind, distant[0], 64:, :],
                            own[low][kind, distant[1], 64:, :],
                            own[k][kind, distant[2], :64, :],
                            own[k][kind, distant[3], :64, :],
                        ],
                        axis=0,
                    ),
                )
            )
            return chunks

        peak = None
        for i, (side, load) in enumerate(rows(0)):
            s = lax.dot_general(query, load(), NT, preferred_element_type=jnp.float32) * EXP2_SCALE + bias[side]
            scores[:, 256 * i : 256 * i + 256] = s
            top = jnp.maximum(s[:, :128], s[:, 128:])
            peak = top if peak is None else jnp.maximum(peak, top)
        peak = jnp.max(peak, axis=1, keepdims=True)
        total = blended = None
        for i, (side, load) in enumerate(rows(1)):
            p = jnp.exp2(scores[:, 256 * i : 256 * i + 256] - peak)
            part = p[:, :128] + p[:, 128:]
            total = part if total is None else total + part
            o = jnp.dot(p.astype(jnp.bfloat16), load(), preferred_element_type=jnp.float32)
            blended = o if blended is None else blended + o
        total = jnp.sum(total, axis=1, keepdims=True)
        result[k, t] = (blended / total).astype(jnp.bfloat16)

    def out_copy(k, t, half):
        slot = (k + 1) % 4 if half == 0 else k
        py = (y + 4 - slot) % 4
        rows = pl.ds(0, 64) if half == 0 else pl.ds(64, 64)
        there = pl.ds(64, 64) if half == 0 else pl.ds(0, 64)
        return (result.at[k, pl.ds(2 * t, 2), rows], out.at[:, there, lanes(x * 4 + y)], o_send.at[(4 * k + t) * 2 + half], py, slot)

    def out_remote(k, t, half):
        src, dst, ss, py, _ = out_copy(k, t, half)
        return pltpu.make_async_remote_copy(src, dst, ss, o_recv, device_id=source(t, py), device_id_type=MESH)

    def give(k, t):
        for half in (0, 1):
            src, dst, _, _, slot = out_copy(k, t, half)
            if slot == 0:
                mine = (t == ta) & (x_hi == core)

                @pl.when(mine)
                def _():
                    pltpu.make_async_copy(src, dst, o_recv).start()

                @pl.when(jnp.logical_not(mine))
                def _():
                    out_remote(k, t, half).start()
            else:
                out_remote(k, t, half).start()

    def given(k, t):
        for half in (0, 1):
            slot = out_copy(k, t, half)[4]
            if slot == 0:

                @pl.when(jnp.logical_not((t == ta) & (x_hi == core)))
                def _():
                    out_remote(k, t, half).wait_send()
            else:
                out_remote(k, t, half).wait_send()

    for k in range(4):
        forward(k)
    arrived(0)
    for k in range(4):
        if k < 3:
            arrived(k + 1)
        set_bias(k)

        @pl.loop(0, 4)
        def _(t):
            @pl.loop(0, 2)
            def _(f):
                unit(k, 2 * t + f)

            give(k, t)

    for k in range(4):
        exchanged(far_copy, k)
        exchanged(kv_copy, k)
        exchanged(q_copy, k)

        @pl.loop(0, 4)
        def _(t):
            @pl.when(has_right)
            def _():
                halo_copy(k, t, 1).wait_send()

            @pl.when(has_left)
            def _():
                halo_copy(k, t, -1).wait_send()

            given(k, t)

    pltpu.make_async_copy(out, out, o_recv).wait()


def per_device(queries, keyvals, far_frames):
    frames, _, _, features = queries.shape
    q = queries.reshape(frames, ROWS, features)
    kv = keyvals.reshape(2, frames, ROWS, features)
    far = far_frames.reshape(-1)
    cells = [pltpu.VMEM((2, NF, ROWS, HD), jnp.bfloat16)] * 12
    dma = pltpu.SemaphoreType.DMA
    out = pl.pallas_call(
        kernel,
        out_shape=jax.ShapeDtypeStruct(q.shape, jnp.bfloat16),
        in_specs=[pl.BlockSpec(memory_space=pl.ANY)] * 2 + [pl.BlockSpec(memory_space=pltpu.SMEM)],
        out_specs=pl.BlockSpec(memory_space=pl.ANY),
        scratch_shapes=[pltpu.VMEM((NF, ROWS, HD), jnp.bfloat16)] * 4
        + cells
        + [
            pltpu.SMEM((16, 8), jnp.int32),
            pltpu.VMEM((4, ROWS, 2 * ROWS), jnp.float32),
            pltpu.VMEM((ROWS, 2560), jnp.float32),
            pltpu.VMEM((ROWS, 2560), jnp.bfloat16),
            pltpu.VMEM((4, NF, ROWS, HD), jnp.bfloat16),
        ]
        + [dma((16,))] * 6
        + [dma((2, 16))] * 2
        + [dma((32,)), dma],
        compiler_params=pltpu.CompilerParams(collective_id=0, has_side_effects=True, vmem_limit_bytes=56 * 2**20),
        name="tile_attention",
    )(q, kv, far)
    return out.reshape(queries.shape)


def solution(mesh):
    placed = (P("ta", "ha", "wa", None), P(None, "ta", "ha", "wa", None), P("ta", "ha", "wa", None))
    return jax.shard_map(per_device, mesh=mesh, in_specs=placed, out_specs=P("ta", "ha", "wa", None), check_vma=False)
```

```python
import functools

import jax
import jax.numpy as jnp
from jax import lax
from jax.experimental import pallas as pl
from jax.experimental.pallas import tpu as pltpu
from jax.sharding import PartitionSpec as P

MESH = pl.DeviceIdType.MESH
HD = 128
NF = 8
ROWS = 128
EXP2_SCALE = HD**-0.5 * 1.4426950408889634
NEG = -1e30
NT = (((1,), (1,)), ((), ()))


def kernel(q, kv, far, out, *scratch):
    qs, own, left, right = (scratch[4 * i : 4 * i + 4] for i in range(4))
    (fars, bias, *held, result, kv_send, kv_recv, q_send, q_recv, f_send, f_recv, z_send, z_recv, o_send, o_recv) = scratch[16:]
    scores, peaks = held[:2], held[2:]
    ta, y, wa = lax.axis_index("ta"), lax.axis_index("ha"), lax.axis_index("wa")
    x_lo, core, x_hi, z = ta // 2, ta % 2, wa // 8, wa % 8
    x = x_hi * 2 + x_lo
    column = core * 8 + z
    has_left, has_right = column > 0, column < 15

    def place(px, pcore, py):
        return {"ta": (px % 2) * 2 + pcore, "ha": py, "wa": (px // 2) * 8 + z}

    def source(pta, py):
        return {"ta": pta, "ha": py, "wa": core * 8 + z}

    def beside(side):
        c = column + side
        return {"ta": x_lo * 2 + c // 8, "ha": y, "wa": x_hi * 8 + c % 8}

    def lanes(head):
        return pl.ds(pl.multiple_of(head * HD, HD), HD)

    barrier = pltpu.get_barrier_semaphore()

    @pl.loop(0, 16)
    def _(i):
        for device in (place(i // 4, x_hi, i % 4), source(i // 4, i % 4)):
            pl.semaphore_signal(barrier, inc=1, device_id=device, device_id_type=MESH)

    for side, there in ((-1, has_left), (1, has_right)):

        @pl.when(there)
        def _(side=side):
            pl.semaphore_signal(barrier, inc=1, device_id=beside(side), device_id_type=MESH)

    pl.semaphore_wait(barrier, 32 + has_left.astype(jnp.int32) + has_right.astype(jnp.int32))

    def kv_copy(k, dx):
        px, py = (x + dx) % 4, (y + k) % 4
        return (kv.at[:, :, :, lanes(px * 4 + py)], own[k].at[:, pl.ds(2 * ta, 2)], kv_send.at[4 * k + dx], kv_recv.at[4 * k + ta], px, py)

    def q_copy(k, dx):
        px, py = (x + dx) % 4, (y + k) % 4
        return (q.at[:, :, lanes(px * 4 + py)], qs[k].at[pl.ds(2 * ta, 2)], q_send.at[4 * k + dx], q_recv.at[4 * k + ta], px, py)

    def far_copy(k, dx):
        px, py = (x + dx) % 4, (y + k) % 4
        return (far, fars.at[4 * k + ta], f_send.at[4 * k + dx], f_recv.at[4 * k + ta], px, py)

    def remote(copy):
        src, dst, ss, rs, px, py = copy
        return pltpu.make_async_remote_copy(src, dst, ss, rs, device_id=place(px, x_hi, py), device_id_type=MESH)

    def exchange(make, *slots):
        for k, steps in ((0, (0, 1, 3, 2)), (1, (0,)), (3, (0,)), (1, (1,)), (3, (3,)), (1, (3,)), (3, (1,)), (1, (2,)), (3, (2,)), (2, (0, 1, 3, 2))):
            for dx in steps if k in slots else ():
                copy = make(k, dx)
                if k == dx == 0:

                    @pl.when(core == x_hi)
                    def _():
                        pltpu.make_async_copy(copy[0], copy[1], copy[3]).start()

                    @pl.when(core != x_hi)
                    def _():
                        remote(copy).start()
                else:
                    remote(copy).start()

    def exchanged(make, k):
        if k == 0:

            @pl.when(core != x_hi)
            def _():
                remote(make(k, 0)).wait_send()
        else:
            remote(make(k, 0)).wait_send()

        @pl.loop(1, 4)
        def _(dx):
            remote(make(k, dx)).wait_send()

    nearer = ((x + 4 - 2 * core) % 4 + 1) % 4 // 2

    def piece(j):
        return ((nearer + j // 2) % 2) * 2 + j % 2

    def halo_copy(k, t, side):
        part = (slice(None), pl.ds(2 * t, 2))
        s = 0 if side < 0 else 1
        return pltpu.make_async_remote_copy(
            own[k].at[part],
            (right if side < 0 else left)[k].at[part],
            z_send.at[s, 4 * k + t],
            z_recv.at[s, 4 * k + t],
            device_id=beside(side),
            device_id_type=MESH,
        )

    def forward(k, first=0, last=4):
        @pl.loop(first, last)
        def _(j):
            t = piece(j)
            pltpu.make_async_copy(own[k].at[:, pl.ds(2 * t, 2)], own[k].at[:, pl.ds(2 * t, 2)], kv_recv.at[4 * k + t]).wait()
            for side, there in ((1, has_right), (-1, has_left)):

                @pl.when(there)
                def _(side=side):
                    halo_copy(k, t, side).start()

    def arrived(k, first=0, last=4):
        @pl.loop(first, last)
        def _(j):
            t = piece(j)

            @pl.when(has_left)
            def _():
                halo_copy(k, t, 1).wait_recv()

            @pl.when(has_right)
            def _():
                halo_copy(k, t, -1).wait_recv()

            pltpu.make_async_copy(qs[k].at[pl.ds(2 * t, 2)], qs[k].at[pl.ds(2 * t, 2)], q_recv.at[4 * k + t]).wait()
            pltpu.make_async_copy(far, fars.at[4 * k + t], f_recv.at[4 * k + t]).wait()

    def set_bias(k, at=0):
        wraps = (y == k).astype(jnp.int32)
        row = lax.broadcasted_iota(jnp.int32, (ROWS, 2 * ROWS), 0)
        key = lax.broadcasted_iota(jnp.int32, (ROWS, 2 * ROWS), 1)
        half = row // 64
        base = jnp.where((key >= half * (64 + 64 * wraps)) & (key < 192 - 64 * wraps + half * 256), 0.0, NEG).astype(jnp.float32)
        bias[at + 1] = base
        bias[at + 0] = jnp.where(has_left, base, NEG)
        bias[at + 2] = jnp.where(has_right, base, NEG)
        bias[at + 3] = jnp.where(half == key // 128, 0.0, NEG).astype(jnp.float32)

    def chunks(k, t, kind):
        low = (k + 1) % 4
        f_low, f_here, f_at = 4 * low + t // 2, 4 * k + t // 2, (t % 2) * 4
        distant = [(low, fars[f_low, f_at + 2], 64), (low, fars[f_low, f_at + 3], 64), (k, fars[f_here, f_at], 0), (k, fars[f_here, f_at + 1], 0)]

        def near(cells, f):
            return lambda: jnp.concatenate([cells[low][kind, f], cells[k][kind, f]], axis=0)

        loads = [(side, near(cells, f)) for side, cells in enumerate((left, own, right)) for f in ((t + 7) % NF, t, (t + 1) % NF)]
        return loads + [(3, lambda: jnp.concatenate([own[s][kind, f, at : at + 64, :] for s, f, at in distant], axis=0))]

    def score(k, t, held, at):
        low = (k + 1) % 4
        query = jnp.concatenate([qs[low][t, 64:, :], qs[k][t, :64, :]], axis=0)
        peak = None
        for i, (side, load) in enumerate(chunks(k, t, 0)):
            s = lax.dot_general(query, load(), NT, preferred_element_type=jnp.float32) * EXP2_SCALE + bias[at + side]
            scores[held][:, 256 * i : 256 * i + 256] = s
            top = jnp.maximum(s[:, :128], s[:, 128:])
            peak = top if peak is None else jnp.maximum(peak, top)
        peaks[held][...] = peak

    def blend(k, t, held):
        peak = jnp.max(peaks[held][...], axis=1, keepdims=True)
        total = blended = None
        for i, (_, load) in enumerate(chunks(k, t, 1)):
            p = jnp.exp2(scores[held][:, 256 * i : 256 * i + 256] - peak)
            part = p[:, :128] + p[:, 128:]
            total = part if total is None else total + part
            o = jnp.dot(p.astype(jnp.bfloat16), load(), preferred_element_type=jnp.float32)
            blended = o if blended is None else blended + o
        total = jnp.sum(total, axis=1, keepdims=True)
        result[k, t] = (blended / total).astype(jnp.bfloat16)

    def units(k, first, at=0):
        for held in (0, 1):
            score(k, (first + held) % NF, held, at)
        for held in (0, 1):
            blend(k, (first + held) % NF, held)

    def out_copy(k, t, half):
        slot = (k + 1) % 4 if half == 0 else k
        py = (y + 4 - slot) % 4
        rows = pl.ds(0, 64) if half == 0 else pl.ds(64, 64)
        there = pl.ds(64, 64) if half == 0 else pl.ds(0, 64)
        return (result.at[k, pl.ds(2 * t, 2), rows], out.at[:, there, lanes(x * 4 + y)], o_send.at[(4 * k + t) * 2 + half], py, slot)

    def out_remote(k, t, half):
        src, dst, ss, py, _ = out_copy(k, t, half)
        return pltpu.make_async_remote_copy(src, dst, ss, o_recv, device_id=source(t, py), device_id_type=MESH)

    def give(k, t):
        for half in (0, 1):
            src, dst, _, _, slot = out_copy(k, t, half)
            if slot == 0:
                mine = (t == ta) & (x_hi == core)

                @pl.when(mine)
                def _():
                    pltpu.make_async_copy(src, dst, o_recv).start()

                @pl.when(jnp.logical_not(mine))
                def _():
                    out_remote(k, t, half).start()
            else:
                out_remote(k, t, half).start()

    def given(k, t):
        for half in (0, 1):
            slot = out_copy(k, t, half)[4]
            if slot == 0:

                @pl.when(jnp.logical_not((t == ta) & (x_hi == core)))
                def _():
                    out_remote(k, t, half).wait_send()
            else:
                out_remote(k, t, half).wait_send()

    exchange(kv_copy, 0)
    exchange(kv_copy, 1, 3)
    exchange(q_copy, 0)
    @pl.when(column == 0)
    def _():
        for ref in left:
            ref[...] = jnp.zeros_like(ref)

    @pl.when(column == 15)
    def _():
        for ref in right:
            ref[...] = jnp.zeros_like(ref)

    forward(0)
    exchange(q_copy, 1, 3)
    exchange(kv_copy, 2)
    forward(1)
    exchange(q_copy, 2)
    exchange(far_copy, 0, 1, 2, 3)
    forward(3)

    def full(k):
        set_bias(k)

        @pl.loop(0, 4)
        def _(t):
            units(k, 2 * t)
            give(k, t)

    forward(2)
    arrived(0)
    arrived(1)
    full(0)
    arrived(3)
    full(3)
    base = 4 * nearer
    set_bias(1, 0)
    set_bias(2, 4)
    arrived(2, 0, 1)

    @pl.loop(1, 4)
    def _(j):
        arrived(2, j, j + 1)
        for k in (1, 2):
            units(k, base + 2 * j - 1, 4 * k - 4)

        @pl.when(j > 1)
        def _():
            for k in (1, 2):
                give(k, piece(j - 1))

    for k in (1, 2):
        units(k, base + 7, 4 * k - 4)
        give(k, piece(3))
        give(k, piece(0))

    for k in range(4):
        exchanged(far_copy, k)
        exchanged(kv_copy, k)
        exchanged(q_copy, k)

        @pl.loop(0, 4)
        def _(t):
            @pl.when(has_right)
            def _():
                halo_copy(k, t, 1).wait_send()

            @pl.when(has_left)
            def _():
                halo_copy(k, t, -1).wait_send()

            given(k, t)

    pltpu.make_async_copy(out, out, o_recv).wait()


def per_device(queries, keyvals, far_frames):
    frames, _, _, features = queries.shape
    q = queries.reshape(frames, ROWS, features)
    kv = keyvals.reshape(2, frames, ROWS, features)
    far = far_frames.reshape(-1)
    cells = [pltpu.VMEM((2, NF, ROWS, HD), jnp.bfloat16)] * 12
    dma = pltpu.SemaphoreType.DMA
    out = pl.pallas_call(
        kernel,
        out_shape=jax.ShapeDtypeStruct(q.shape, jnp.bfloat16),
        in_specs=[pl.BlockSpec(memory_space=pl.ANY)] * 2 + [pl.BlockSpec(memory_space=pltpu.SMEM)],
        out_specs=pl.BlockSpec(memory_space=pl.ANY),
        scratch_shapes=[pltpu.VMEM((NF, ROWS, HD), jnp.bfloat16)] * 4
        + cells
        + [
            pltpu.SMEM((16, 8), jnp.int32),
            pltpu.VMEM((8, ROWS, 2 * ROWS), jnp.float32),
            pltpu.VMEM((ROWS, 2560), jnp.float32),
            pltpu.VMEM((ROWS, 2560), jnp.float32),
            pltpu.VMEM((ROWS, HD), jnp.float32),
            pltpu.VMEM((ROWS, HD), jnp.float32),
            pltpu.VMEM((4, NF, ROWS, HD), jnp.bfloat16),
        ]
        + [dma((16,))] * 6
        + [dma((2, 16))] * 2
        + [dma((32,)), dma],
        compiler_params=pltpu.CompilerParams(collective_id=0, has_side_effects=True, vmem_limit_bytes=56 * 2**20),
        name="tile_attention",
    )(q, kv, far)
    return out.reshape(queries.shape)


def solution(mesh):
    placed = (P("ta", "ha", "wa", None), P(None, "ta", "ha", "wa", None), P("ta", "ha", "wa", None))
    return jax.shard_map(per_device, mesh=mesh, in_specs=placed, out_specs=P("ta", "ha", "wa", None), check_vma=False)
```

```python
import functools

import jax
import jax.numpy as jnp
from jax import lax
from jax.experimental import pallas as pl
from jax.experimental.pallas import tpu as pltpu
from jax.sharding import PartitionSpec as P

MESH = pl.DeviceIdType.MESH
HD = 128
NF = 8
ROWS = 128
EXP2_SCALE = HD**-0.5 * 1.4426950408889634
NEG = -1e30
NT = (((1,), (1,)), ((), ()))


def kernel(q, kv, far, out, *scratch):
    qs, own, left, right = (scratch[4 * i : 4 * i + 4] for i in range(4))
    (fars, bias, *held, result, kv_send, kv_recv, q_send, q_recv, f_send, f_recv, z_send, z_recv, o_send, o_recv) = scratch[16:]
    scores, peaks = held[:2], held[2:]
    ta, y, wa = lax.axis_index("ta"), lax.axis_index("ha"), lax.axis_index("wa")
    x_lo, core, x_hi, z = ta // 2, ta % 2, wa // 8, wa % 8
    x = x_hi * 2 + x_lo
    column = core * 8 + z
    has_left, has_right = column > 0, column < 15

    def place(px, pcore, py):
        return {"ta": (px % 2) * 2 + pcore, "ha": py, "wa": (px // 2) * 8 + z}

    def source(pta, py):
        return {"ta": pta, "ha": py, "wa": core * 8 + z}

    def beside(side):
        c = column + side
        return {"ta": x_lo * 2 + c // 8, "ha": y, "wa": x_hi * 8 + c % 8}

    def lanes(head):
        return pl.ds(pl.multiple_of(head * HD, HD), HD)

    barrier = pltpu.get_barrier_semaphore()

    @pl.loop(0, 16)
    def _(i):
        for device in (place(i // 4, x_hi, i % 4), source(i // 4, i % 4)):
            pl.semaphore_signal(barrier, inc=1, device_id=device, device_id_type=MESH)

    for side, there in ((-1, has_left), (1, has_right)):

        @pl.when(there)
        def _(side=side):
            pl.semaphore_signal(barrier, inc=1, device_id=beside(side), device_id_type=MESH)

    pl.semaphore_wait(barrier, 32 + has_left.astype(jnp.int32) + has_right.astype(jnp.int32))

    def kv_copy(k, dx):
        px, py = (x + dx) % 4, (y + k) % 4
        return (kv.at[:, :, :, lanes(px * 4 + py)], own[k].at[:, pl.ds(2 * ta, 2)], kv_send.at[4 * k + dx], kv_recv.at[4 * k + ta], px, py)

    def q_copy(k, dx):
        px, py = (x + dx) % 4, (y + k) % 4
        return (q.at[:, :, lanes(px * 4 + py)], qs[k].at[pl.ds(2 * ta, 2)], q_send.at[4 * k + dx], q_recv.at[4 * k + ta], px, py)

    def far_copy(k, dx):
        px, py = (x + dx) % 4, (y + k) % 4
        return (far, fars.at[4 * k + ta], f_send.at[4 * k + dx], f_recv.at[4 * k + ta], px, py)

    def remote(copy):
        src, dst, ss, rs, px, py = copy
        return pltpu.make_async_remote_copy(src, dst, ss, rs, device_id=place(px, x_hi, py), device_id_type=MESH)

    def exchange(make, *slots):
        for k, steps in ((0, (0, 1, 3, 2)), (1, (0,)), (3, (0,)), (1, (1,)), (3, (3,)), (1, (3,)), (3, (1,)), (1, (2,)), (3, (2,)), (2, (0, 1, 3, 2))):
            for dx in steps if k in slots else ():
                copy = make(k, dx)
                if k == dx == 0:

                    @pl.when(core == x_hi)
                    def _():
                        pltpu.make_async_copy(copy[0], copy[1], copy[3]).start()

                    @pl.when(core != x_hi)
                    def _():
                        remote(copy).start()
                else:
                    remote(copy).start()

    def exchanged(make, k):
        if k == 0:

            @pl.when(core != x_hi)
            def _():
                remote(make(k, 0)).wait_send()
        else:
            remote(make(k, 0)).wait_send()

        @pl.loop(1, 4)
        def _(dx):
            remote(make(k, dx)).wait_send()

    nearer = ((x + 4 - 2 * core) % 4 + 1) % 4 // 2

    def piece(j):
        return ((nearer + j // 2) % 2) * 2 + j % 2

    def halo_copy(k, t, side):
        part = (slice(None), pl.ds(2 * t, 2))
        s = 0 if side < 0 else 1
        return pltpu.make_async_remote_copy(
            own[k].at[part],
            (right if side < 0 else left)[k].at[part],
            z_send.at[s, 4 * k + t],
            z_recv.at[s, 4 * k + t],
            device_id=beside(side),
            device_id_type=MESH,
        )

    def forward(k, first=0, last=4):
        @pl.loop(first, last)
        def _(j):
            t = piece(j)
            pltpu.make_async_copy(own[k].at[:, pl.ds(2 * t, 2)], own[k].at[:, pl.ds(2 * t, 2)], kv_recv.at[4 * k + t]).wait()
            for side, there in ((1, has_right), (-1, has_left)):

                @pl.when(there)
                def _(side=side):
                    halo_copy(k, t, side).start()

    def arrived(k, first=0, last=4):
        @pl.loop(first, last)
        def _(j):
            t = piece(j)

            @pl.when(has_left)
            def _():
                halo_copy(k, t, 1).wait_recv()

            @pl.when(has_right)
            def _():
                halo_copy(k, t, -1).wait_recv()

            pltpu.make_async_copy(qs[k].at[pl.ds(2 * t, 2)], qs[k].at[pl.ds(2 * t, 2)], q_recv.at[4 * k + t]).wait()
            pltpu.make_async_copy(far, fars.at[4 * k + t], f_recv.at[4 * k + t]).wait()

    def set_bias(k, at=0):
        wraps = (y == k).astype(jnp.int32)
        row = lax.broadcasted_iota(jnp.int32, (ROWS, 2 * ROWS), 0)
        key = lax.broadcasted_iota(jnp.int32, (ROWS, 2 * ROWS), 1)
        half = row // 64
        base = jnp.where((key >= half * (64 + 64 * wraps)) & (key < 192 - 64 * wraps + half * 256), 0.0, NEG).astype(jnp.float32)
        bias[at + 1] = base
        bias[at + 0] = jnp.where(has_left, base, NEG)
        bias[at + 2] = jnp.where(has_right, base, NEG)
        bias[at + 3] = jnp.where(half == key // 128, 0.0, NEG).astype(jnp.float32)

    def chunks(k, t, kind):
        low = (k + 1) % 4
        f_low, f_here, f_at = 4 * low + t // 2, 4 * k + t // 2, (t % 2) * 4
        distant = [(low, fars[f_low, f_at + 2], 64), (low, fars[f_low, f_at + 3], 64), (k, fars[f_here, f_at], 0), (k, fars[f_here, f_at + 1], 0)]

        def near(cells, f):
            return lambda: jnp.concatenate([cells[low][kind, f], cells[k][kind, f]], axis=0)

        loads = [(side, near(cells, f)) for side, cells in enumerate((left, own, right)) for f in ((t + 7) % NF, t, (t + 1) % NF)]
        return loads + [(3, lambda: jnp.concatenate([own[s][kind, f, at : at + 64, :] for s, f, at in distant], axis=0))]

    def score(k, t, held, at):
        low = (k + 1) % 4
        query = jnp.concatenate([qs[low][t, 64:, :], qs[k][t, :64, :]], axis=0)
        peak = None
        for i, (side, load) in enumerate(chunks(k, t, 0)):
            s = lax.dot_general(query, load(), NT, preferred_element_type=jnp.float32) * EXP2_SCALE + bias[at + side]
            scores[held][:, 256 * i : 256 * i + 256] = s
            top = jnp.maximum(s[:, :128], s[:, 128:])
            peak = top if peak is None else jnp.maximum(peak, top)
        peaks[held][...] = peak

    def blend(k, t, held):
        peak = jnp.max(peaks[held][...], axis=1, keepdims=True)
        total = blended = None
        for i, (_, load) in enumerate(chunks(k, t, 1)):
            p = jnp.exp2(scores[held][:, 256 * i : 256 * i + 256] - peak)
            part = p[:, :128] + p[:, 128:]
            total = part if total is None else total + part
            o = jnp.dot(p.astype(jnp.bfloat16), load(), preferred_element_type=jnp.float32)
            blended = o if blended is None else blended + o
        total = jnp.sum(total, axis=1, keepdims=True)
        result[k, t] = (blended / total).astype(jnp.bfloat16)

    def units(k, first, at=0):
        for held in (0, 1):
            score(k, (first + held) % NF, held, at)
        for held in (0, 1):
            blend(k, (first + held) % NF, held)

    def out_copy(k, f, count, half):
        slot = (k + 1) % 4 if half == 0 else k
        py = (y + 4 - slot) % 4
        rows = pl.ds(0, 64) if half == 0 else pl.ds(64, 64)
        there = pl.ds(64, 64) if half == 0 else pl.ds(0, 64)
        return (
            result.at[k, pl.ds(f, count), rows],
            out.at[pl.ds(f % 2, count), there, lanes(x * 4 + y)],
            o_send.at[(4 * k + f // 2) * 2 + half],
            py,
            slot,
        )

    def out_remote(k, f, count, half):
        src, dst, ss, py, _ = out_copy(k, f, count, half)
        return pltpu.make_async_remote_copy(src, dst, ss, o_recv, device_id=source(f // 2, py), device_id_type=MESH)

    def give(k, f, count):
        for half in (0, 1):
            src, dst, _, _, slot = out_copy(k, f, count, half)
            if slot == 0:
                mine = (f // 2 == ta) & (x_hi == core)

                @pl.when(mine)
                def _():
                    pltpu.make_async_copy(src, dst, o_recv).start()

                @pl.when(jnp.logical_not(mine))
                def _():
                    out_remote(k, f, count, half).start()
            else:
                out_remote(k, f, count, half).start()

    def given(k, t):
        for half in (0, 1):
            slot = out_copy(k, 2 * t, 2, half)[4]
            if slot == 0:

                @pl.when(jnp.logical_not((t == ta) & (x_hi == core)))
                def _():
                    out_remote(k, 2 * t, 2, half).wait_send()
            else:
                out_remote(k, 2 * t, 2, half).wait_send()

    def full(k):
        set_bias(k)

        @pl.loop(0, 4)
        def _(t):
            units(k, 2 * t)
            give(k, 2 * t, 2)

    exchange(kv_copy, 0)
    exchange(far_copy, 0, 1, 2, 3)
    exchange(kv_copy, 1,3)
    @pl.when(column == 0)
    def _():
        for ref in left:
            ref[...] = jnp.zeros_like(ref)

    @pl.when(column == 15)
    def _():
        for ref in right:
            ref[...] = jnp.zeros_like(ref)

    forward(0)
    exchange(kv_copy, 2)
    exchange(q_copy, 0)
    forward(1)
    exchange(q_copy, 1,3)
    forward(3)
    exchange(q_copy, 2)
    arrived(0)
    arrived(1)
    set_bias(0)

    @pl.loop(0, 4)
    def _(t):
        forward(2, t, t + 1)
        units(0, 2 * t)
        give(0, 2 * t, 2)

    arrived(3)
    full(3)
    base = 4 * nearer
    set_bias(1, 0)
    set_bias(2, 4)
    arrived(2, 0, 1)

    def follow(first):
        for k in (1, 2):
            units(k, first, 4 * k - 4)
            for held in (0, 1):
                give(k, (first + held) % NF, 1)

    @pl.loop(1, 4)
    def _(j):
        arrived(2, j, j + 1)
        follow(base + 2 * j - 1)

    follow(base + 7)

    for k in range(4):
        exchanged(far_copy, k)
        exchanged(kv_copy, k)
        exchanged(q_copy, k)

        @pl.loop(0, 4)
        def _(t):
            @pl.when(has_right)
            def _():
                halo_copy(k, t, 1).wait_send()

            @pl.when(has_left)
            def _():
                halo_copy(k, t, -1).wait_send()

            given(k, t)

    pltpu.make_async_copy(out, out, o_recv).wait()


def per_device(queries, keyvals, far_frames):
    frames, _, _, features = queries.shape
    q = queries.reshape(frames, ROWS, features)
    kv = keyvals.reshape(2, frames, ROWS, features)
    far = far_frames.reshape(-1)
    cells = [pltpu.VMEM((2, NF, ROWS, HD), jnp.bfloat16)] * 12
    dma = pltpu.SemaphoreType.DMA
    out = pl.pallas_call(
        kernel,
        out_shape=jax.ShapeDtypeStruct(q.shape, jnp.bfloat16),
        in_specs=[pl.BlockSpec(memory_space=pl.ANY)] * 2 + [pl.BlockSpec(memory_space=pltpu.SMEM)],
        out_specs=pl.BlockSpec(memory_space=pl.ANY),
        scratch_shapes=[pltpu.VMEM((NF, ROWS, HD), jnp.bfloat16)] * 4
        + cells
        + [
            pltpu.SMEM((16, 8), jnp.int32),
            pltpu.VMEM((8, ROWS, 2 * ROWS), jnp.float32),
            pltpu.VMEM((ROWS, 2560), jnp.float32),
            pltpu.VMEM((ROWS, 2560), jnp.float32),
            pltpu.VMEM((ROWS, HD), jnp.float32),
            pltpu.VMEM((ROWS, HD), jnp.float32),
            pltpu.VMEM((4, NF, ROWS, HD), jnp.bfloat16),
        ]
        + [dma((16,))] * 6
        + [dma((2, 16))] * 2
        + [dma((32,)), dma],
        compiler_params=pltpu.CompilerParams(collective_id=0, has_side_effects=True, vmem_limit_bytes=56 * 2**20),
        name="tile_attention",
    )(q, kv, far)
    return out.reshape(queries.shape)


def solution(mesh):
    placed = (P("ta", "ha", "wa", None), P(None, "ta", "ha", "wa", None), P("ta", "ha", "wa", None))
    return jax.shard_map(per_device, mesh=mesh, in_specs=placed, out_specs=P("ta", "ha", "wa", None), check_vma=False)
```

```python
import functools

import jax
import jax.numpy as jnp
from jax import lax
from jax.experimental import pallas as pl
from jax.experimental.pallas import tpu as pltpu
from jax.sharding import PartitionSpec as P

MESH = pl.DeviceIdType.MESH
HD = 128
NF = 8
ROWS = 128
EXP2_SCALE = HD**-0.5 * 1.4426950408889634
NEG = -1e30
NT = (((1,), (1,)), ((), ()))


def kernel(q, kv, far, out, *scratch):
    qs, own, left, right = (scratch[4 * i : 4 * i + 4] for i in range(4))
    (fars, bias, *held, result, kv_send, kv_recv, q_send, q_recv, f_send, f_recv, z_send, z_recv, o_send, o_recv) = scratch[16:]
    scores, peaks = held[:4], held[4:]
    ta, y, wa = lax.axis_index("ta"), lax.axis_index("ha"), lax.axis_index("wa")
    x_lo, core, x_hi, z = ta // 2, ta % 2, wa // 8, wa % 8
    x = x_hi * 2 + x_lo
    column = core * 8 + z
    has_left, has_right = column > 0, column < 15

    def place(px, pcore, py):
        return {"ta": (px % 2) * 2 + pcore, "ha": py, "wa": (px // 2) * 8 + z}

    def source(pta, py):
        return {"ta": pta, "ha": py, "wa": core * 8 + z}

    def beside(side):
        c = column + side
        return {"ta": x_lo * 2 + c // 8, "ha": y, "wa": x_hi * 8 + c % 8}

    def lanes(head):
        return pl.ds(pl.multiple_of(head * HD, HD), HD)

    barrier = pltpu.get_barrier_semaphore()

    @pl.loop(0, 16)
    def _(i):
        for device in (place(i // 4, x_hi, i % 4), source(i // 4, i % 4)):
            pl.semaphore_signal(barrier, inc=1, device_id=device, device_id_type=MESH)

    for side, there in ((-1, has_left), (1, has_right)):

        @pl.when(there)
        def _(side=side):
            pl.semaphore_signal(barrier, inc=1, device_id=beside(side), device_id_type=MESH)

    pl.semaphore_wait(barrier, 32 + has_left.astype(jnp.int32) + has_right.astype(jnp.int32))

    def kv_copy(k, dx):
        px, py = (x + dx) % 4, (y + k) % 4
        return (kv.at[:, :, :, lanes(px * 4 + py)], own[k].at[:, pl.ds(2 * ta, 2)], kv_send.at[4 * k + dx], kv_recv.at[4 * k + ta], px, py)

    def q_copy(k, dx):
        px, py = (x + dx) % 4, (y + k) % 4
        return (q.at[:, :, lanes(px * 4 + py)], qs[k].at[pl.ds(2 * ta, 2)], q_send.at[4 * k + dx], q_recv.at[4 * k + ta], px, py)

    def far_copy(k, dx):
        px, py = (x + dx) % 4, (y + k) % 4
        return (far, fars.at[4 * k + ta], f_send.at[4 * k + dx], f_recv.at[4 * k + ta], px, py)

    def remote(copy):
        src, dst, ss, rs, px, py = copy
        return pltpu.make_async_remote_copy(src, dst, ss, rs, device_id=place(px, x_hi, py), device_id_type=MESH)

    def exchange(make, *slots):
        for k, steps in ((0, (0, 1, 3, 2)), (1, (0,)), (3, (0,)), (1, (1,)), (3, (3,)), (1, (3,)), (3, (1,)), (1, (2,)), (3, (2,)), (2, (0, 1, 3, 2))):
            for dx in steps if k in slots else ():
                copy = make(k, dx)
                if k == dx == 0:

                    @pl.when(core == x_hi)
                    def _():
                        pltpu.make_async_copy(copy[0], copy[1], copy[3]).start()

                    @pl.when(core != x_hi)
                    def _():
                        remote(copy).start()
                else:
                    remote(copy).start()

    def exchanged(make, k):
        if k == 0:

            @pl.when(core != x_hi)
            def _():
                remote(make(k, 0)).wait_send()
        else:
            remote(make(k, 0)).wait_send()

        @pl.loop(1, 4)
        def _(dx):
            remote(make(k, dx)).wait_send()

    nearer = ((x + 4 - 2 * core) % 4 + 1) % 4 // 2

    def piece(j):
        return ((nearer + j // 2) % 2) * 2 + j % 2

    def halo_copy(k, t, side):
        part = (slice(None), pl.ds(2 * t, 2))
        s = 0 if side < 0 else 1
        return pltpu.make_async_remote_copy(
            own[k].at[part],
            (right if side < 0 else left)[k].at[part],
            z_send.at[s, 4 * k + t],
            z_recv.at[s, 4 * k + t],
            device_id=beside(side),
            device_id_type=MESH,
        )

    def forward(k, first=0, last=4):
        @pl.loop(first, last)
        def _(j):
            t = piece(j)
            pltpu.make_async_copy(own[k].at[:, pl.ds(2 * t, 2)], own[k].at[:, pl.ds(2 * t, 2)], kv_recv.at[4 * k + t]).wait()
            for side, there in ((1, has_right), (-1, has_left)):

                @pl.when(there)
                def _(side=side):
                    halo_copy(k, t, side).start()

    def arrived(k, first=0, last=4):
        @pl.loop(first, last)
        def _(j):
            t = piece(j)

            @pl.when(has_left)
            def _():
                halo_copy(k, t, 1).wait_recv()

            @pl.when(has_right)
            def _():
                halo_copy(k, t, -1).wait_recv()

            pltpu.make_async_copy(qs[k].at[pl.ds(2 * t, 2)], qs[k].at[pl.ds(2 * t, 2)], q_recv.at[4 * k + t]).wait()
            pltpu.make_async_copy(far, fars.at[4 * k + t], f_recv.at[4 * k + t]).wait()

    def set_bias(k, at=0):
        wraps = (y == k).astype(jnp.int32)
        row = lax.broadcasted_iota(jnp.int32, (ROWS, 2 * ROWS), 0)
        key = lax.broadcasted_iota(jnp.int32, (ROWS, 2 * ROWS), 1)
        half = row // 64
        base = jnp.where((key >= half * (64 + 64 * wraps)) & (key < 192 - 64 * wraps + half * 256), 0.0, NEG).astype(jnp.float32)
        bias[at + 1] = base
        bias[at + 0] = jnp.where(has_left, base, NEG)
        bias[at + 2] = jnp.where(has_right, base, NEG)
        bias[at + 3] = jnp.where(half == key // 128, 0.0, NEG).astype(jnp.float32)

    def chunks(k, t, kind):
        low = (k + 1) % 4
        f_low, f_here, f_at = 4 * low + t // 2, 4 * k + t // 2, (t % 2) * 4
        distant = [(low, fars[f_low, f_at + 2], 64), (low, fars[f_low, f_at + 3], 64), (k, fars[f_here, f_at], 0), (k, fars[f_here, f_at + 1], 0)]

        def near(cells, f):
            return lambda: jnp.concatenate([cells[low][kind, f], cells[k][kind, f]], axis=0)

        loads = [(side, near(cells, f)) for side, cells in enumerate((left, own, right)) for f in ((t + 7) % NF, t, (t + 1) % NF)]
        return loads + [(3, lambda: jnp.concatenate([own[s][kind, f, at : at + 64, :] for s, f, at in distant], axis=0))]

    def score(k, t, held, at):
        low = (k + 1) % 4
        query = jnp.concatenate([qs[low][t, 64:, :], qs[k][t, :64, :]], axis=0)
        peak = None
        for i, (side, load) in enumerate(chunks(k, t, 0)):
            s = lax.dot_general(query, load(), NT, preferred_element_type=jnp.float32) * EXP2_SCALE + bias[at + side]
            scores[held][:, 256 * i : 256 * i + 256] = s
            top = jnp.maximum(s[:, :128], s[:, 128:])
            peak = top if peak is None else jnp.maximum(peak, top)
        peaks[held][...] = peak

    def blend(k, t, held):
        peak = jnp.max(peaks[held][...], axis=1, keepdims=True)
        total = blended = None
        for i, (_, load) in enumerate(chunks(k, t, 1)):
            p = jnp.exp2(scores[held][:, 256 * i : 256 * i + 256] - peak)
            part = p[:, :128] + p[:, 128:]
            total = part if total is None else total + part
            o = jnp.dot(p.astype(jnp.bfloat16), load(), preferred_element_type=jnp.float32)
            blended = o if blended is None else blended + o
        total = jnp.sum(total, axis=1, keepdims=True)
        result[k, t] = (blended / total).astype(jnp.bfloat16)

    def units(k, first, at=0):
        for held in (0, 1):
            score(k, (first + held) % NF, held, at)
        for held in (0, 1):
            blend(k, (first + held) % NF, held)

    def out_copy(k, f, count, half):
        slot = (k + 1) % 4 if half == 0 else k
        py = (y + 4 - slot) % 4
        rows = pl.ds(0, 64) if half == 0 else pl.ds(64, 64)
        there = pl.ds(64, 64) if half == 0 else pl.ds(0, 64)
        return (
            result.at[k, pl.ds(f, count), rows],
            out.at[pl.ds(f % 2, count), there, lanes(x * 4 + y)],
            o_send.at[(4 * k + f // 2) * 2 + half],
            py,
            slot,
        )

    def out_remote(k, f, count, half):
        src, dst, ss, py, _ = out_copy(k, f, count, half)
        return pltpu.make_async_remote_copy(src, dst, ss, o_recv, device_id=source(f // 2, py), device_id_type=MESH)

    def give(k, f, count):
        for half in (0, 1):
            src, dst, _, _, slot = out_copy(k, f, count, half)
            if slot == 0:
                mine = (f // 2 == ta) & (x_hi == core)

                @pl.when(mine)
                def _():
                    pltpu.make_async_copy(src, dst, o_recv).start()

                @pl.when(jnp.logical_not(mine))
                def _():
                    out_remote(k, f, count, half).start()
            else:
                out_remote(k, f, count, half).start()

    def given(k, t):
        for half in (0, 1):
            slot = out_copy(k, 2 * t, 2, half)[4]
            if slot == 0:

                @pl.when(jnp.logical_not((t == ta) & (x_hi == core)))
                def _():
                    out_remote(k, 2 * t, 2, half).wait_send()
            else:
                out_remote(k, 2 * t, 2, half).wait_send()

    def full(k):
        set_bias(k)

        @pl.loop(0, 2)
        def _(i):
            for f in range(4):
                score(k, 4 * i + f, f, 0)
            for f in range(4):
                blend(k, 4 * i + f, f)
            give(k, 4 * i, 2)
            give(k, 4 * i + 2, 2)

    exchange(kv_copy, 0)
    exchange(far_copy, 0, 1, 2, 3)
    exchange(kv_copy, 1,3)
    @pl.when(column == 0)
    def _():
        for ref in left:
            ref[...] = jnp.zeros_like(ref)

    @pl.when(column == 15)
    def _():
        for ref in right:
            ref[...] = jnp.zeros_like(ref)

    forward(0)
    exchange(kv_copy, 2)
    exchange(q_copy, 0)
    forward(1)
    exchange(q_copy, 1,3)
    forward(3)
    exchange(q_copy, 2)
    arrived(0)
    arrived(1)
    set_bias(0)

    @pl.loop(0, 4)
    def _(t):
        forward(2, t, t + 1)
        units(0, 2 * t)
        give(0, 2 * t, 2)

    arrived(3)
    full(3)
    base = 4 * nearer
    set_bias(1, 0)
    set_bias(2, 4)
    arrived(2, 0, 1)

    def follow(first):
        steps = [(k, (first + f) % NF, 2 * k - 2 + f) for k in (1, 2) for f in (0, 1)]
        for k, f, held in steps:
            score(k, f, held, 4 * k - 4)
        for k, f, held in steps:
            blend(k, f, held)
        for k, f, _ in steps:
            give(k, f, 1)

    @pl.loop(1, 4)
    def _(j):
        arrived(2, j, j + 1)
        follow(base + 2 * j - 1)

    follow(base + 7)

    for k in range(4):
        exchanged(far_copy, k)
        exchanged(kv_copy, k)
        exchanged(q_copy, k)

        @pl.loop(0, 4)
        def _(t):
            @pl.when(has_right)
            def _():
                halo_copy(k, t, 1).wait_send()

            @pl.when(has_left)
            def _():
                halo_copy(k, t, -1).wait_send()

            given(k, t)

    pltpu.make_async_copy(out, out, o_recv).wait()


def per_device(queries, keyvals, far_frames):
    frames, _, _, features = queries.shape
    q = queries.reshape(frames, ROWS, features)
    kv = keyvals.reshape(2, frames, ROWS, features)
    far = far_frames.reshape(-1)
    cells = [pltpu.VMEM((2, NF, ROWS, HD), jnp.bfloat16)] * 12
    dma = pltpu.SemaphoreType.DMA
    out = pl.pallas_call(
        kernel,
        out_shape=jax.ShapeDtypeStruct(q.shape, jnp.bfloat16),
        in_specs=[pl.BlockSpec(memory_space=pl.ANY)] * 2 + [pl.BlockSpec(memory_space=pltpu.SMEM)],
        out_specs=pl.BlockSpec(memory_space=pl.ANY),
        scratch_shapes=[pltpu.VMEM((NF, ROWS, HD), jnp.bfloat16)] * 4
        + cells
        + [
            pltpu.SMEM((16, 8), jnp.int32),
            pltpu.VMEM((8, ROWS, 2 * ROWS), jnp.float32),
            *[pltpu.VMEM((ROWS, 2560), jnp.float32)] * 4,
            *[pltpu.VMEM((ROWS, HD), jnp.float32)] * 4,
            pltpu.VMEM((4, NF, ROWS, HD), jnp.bfloat16),
        ]
        + [dma((16,))] * 6
        + [dma((2, 16))] * 2
        + [dma((32,)), dma],
        compiler_params=pltpu.CompilerParams(collective_id=0, has_side_effects=True, vmem_limit_bytes=56 * 2**20),
        name="tile_attention",
    )(q, kv, far)
    return out.reshape(queries.shape)


def solution(mesh):
    placed = (P("ta", "ha", "wa", None), P(None, "ta", "ha", "wa", None), P("ta", "ha", "wa", None))
    return jax.shard_map(per_device, mesh=mesh, in_specs=placed, out_specs=P("ta", "ha", "wa", None), check_vma=False)
```
